512 devices in a mesh: gx: 8 (over y, z_hi), gy: 8 (over x, core), gz: 8 (over z_lo).
Axes of the slice: x: 4, y: 4, z: 16 (z_hi: 2, z_lo: 8; z = z_hi * 8 + z_lo), core: 2. Of those that a mesh axis runs over, the one named last changes fastest.
Arguments:
- gradients: bfloat16 [524288, 128], P(('gx', 'gy', 'gz')), may hold values from -4 to 4
- row_ids: int32 [524288], P(('gx', 'gy', 'gz')), may hold values from 0 to 131071, as said below
- hot_ids: int32 [1024], replicated, may hold values from 0 to 131071, as said below
- embedding: float32 [131072, 128], P(('gx', 'gy', 'gz')), may hold values from -4 to 4
- moments: float32 [131072, 128], P(('gx', 'gy', 'gz')), may hold values from 0.5 to 4
- hot_table: float32 [1024, 128], replicated, may hold values from -4 to 4
- hot_moments: float32 [1024, 128], replicated, may hold values from 4 to 64
Outputs:
- new_table: float32 [131072, 128], P(('gx', 'gy', 'gz'))
- new_moments: float32 [131072, 128], P(('gx', 'gy', 'gz'))
- new_hot_table: float32 [1024, 128], replicated
- new_hot_moments: float32 [1024, 128], replicated
The draws below stay inside these ranges and needn't reach their ends.
Inputs may be any that keep to these rules, and one draw needn't show every extreme that they name: `row_ids`: for each device, its row ids that are not in hot_ids fall on at most 4 distinct rows of any one owner's range of 256 rows (owner = id // 256, devices in the order gx, gy, gz); in every draw some owner gets exactly 4 such distinct ids from every device. `hot_ids`: 1024 distinct ids.
All inputs are finite; a program needn't handle non-finite values.
Results may differ from the reference program's by a relative error of at most 0.0003.
Values sent between devices are 32-bit elements; how exact they have to be, the bound alone decides.
A program may use at most 64 MiB of HBM per device.

```python
import math
import jax
import jax.numpy as jnp

E = 128
TOK_DEV = 1024
ROWS_DEV = 256
HOT = 1024
CAP = 4
ROWS = 131072
TOKENS = 524288
DEVICES = 512


def common_draw(key):
    half_rows = ROWS_DEV // 2
    streams = jax.random.split(key, 12)
    row_keys = jax.random.split(streams[10], DEVICES)
    arrangement = jax.vmap(lambda single: jax.random.permutation(single, ROWS_DEV))(row_keys).astype(jnp.int32)
    owner_base = (jnp.arange(DEVICES, dtype=jnp.int32) * ROWS_DEV)[:, None]
    eligible = (arrangement[:, :half_rows] + owner_base).reshape(-1)
    spare_rows = arrangement[:, half_rows:] + owner_base
    chosen = jax.random.permutation(streams[11], DEVICES * half_rows)[:HOT].astype(jnp.int32)
    frequent = eligible[chosen]
    choose_kind = jax.random.randint(streams[2], (DEVICES, TOK_DEV), 0, 8)
    first_pick = jax.random.randint(streams[3], (DEVICES, TOK_DEV), 0, HOT)
    second_pick = jax.random.randint(streams[4], (DEVICES, TOK_DEV), 0, HOT)
    hot_pick = jnp.minimum(first_pick, second_pick)
    owner_pick = jax.random.randint(streams[5], (DEVICES, TOK_DEV), 0, DEVICES)
    slot_pick = jax.random.randint(streams[6], (DEVICES, TOK_DEV), 0, CAP)
    starts = jax.random.randint(streams[7], (DEVICES, DEVICES), 0, half_rows)
    chosen_owner = jax.random.randint(streams[8], (), 0, DEVICES)
    position = jnp.arange(TOK_DEV)[None, :]
    forced = position < CAP
    owner_pick = jnp.where(forced, chosen_owner, owner_pick)
    slot_pick = jnp.where(forced, position, slot_pick)
    choose_kind = jnp.where(forced, 1, choose_kind)
    offsets = jnp.take_along_axis(starts, owner_pick, axis=1)
    spare_index = (offsets + slot_pick) % half_rows
    infrequent = spare_rows[owner_pick, spare_index]
    picked = jnp.where(choose_kind == 0, frequent[hot_pick], infrequent)
    shuffle_keys = jax.random.split(streams[9], DEVICES)
    shuffles = jax.vmap(lambda single: jax.random.permutation(single, TOK_DEV))(shuffle_keys)
    picked = jnp.take_along_axis(picked, shuffles, axis=1)
    return (frequent.astype(jnp.int32), picked.reshape(-1).astype(jnp.int32))


def draw_row_ids(key, part):
    return common_draw(jax.random.fold_in(key, 7))[1]


def draw_hot_ids(key, part):
    return common_draw(jax.random.fold_in(key, 7))[0]


def levels(rng, extent, pieces, low, high):
    def one(dim, shards_of):
        steps = jax.random.uniform(jax.random.fold_in(jax.random.fold_in(rng, 6), dim), (shards_of,), jnp.float32, low / len(pieces), high / len(pieces))
        return jnp.repeat(jnp.exp(steps), extent[dim] // shards_of).reshape((-1,) + (1,) * (len(extent) - dim - 1))

    level = one(*pieces[0])
    for cut in pieces[1:]:
        level = level * one(*cut)
    return level


def normal_values(stream_key, extent, scale, most, cuts=(), kind=jnp.bfloat16):
    drawn = jax.random.normal(stream_key, extent, jnp.float32) * scale
    if len(cuts) > 0:
        drawn = levels(stream_key, extent, cuts, -0.22, 0.18) * drawn
    return jnp.clip(drawn, min=-most, max=most).astype(kind)


def setup_inputs(seed: int = 0) -> dict:
    seeds = jax.random.split(jax.random.key(seed), 8)
    return {
        "gradients": normal_values(seeds[0], (TOKENS, E), 0.5, 4.0, ((0, 512),)),
        "row_ids": draw_row_ids(jax.random.fold_in(seeds[7], 71), 0),
        "hot_ids": draw_hot_ids(jax.random.fold_in(seeds[7], 71), 0),
        "embedding": normal_values(seeds[3], (ROWS, E), 0.5, 4.0, ((0, 512),), jnp.float32),
        "moments": jnp.clip(jnp.exp(math.log(4.0) - 2.0794415 * jax.random.uniform(seeds[4], (ROWS, E), jnp.float32) ** levels(seeds[4], (ROWS, E), ((0, 512),), -0.2, 0.2)), 0.5, 4.0),
        "hot_table": normal_values(seeds[5], (HOT, E), 0.5, 4.0, (), jnp.float32),
        "hot_moments": jnp.clip(jnp.exp(jax.random.uniform(seeds[6], (HOT, E), jnp.float32, math.log(4.0), math.log(64.0))), 4.0, 64.0),
    }


def adagrad(weights, moments, gradient):
    updated = moments + gradient * gradient
    return (weights - 0.5 * gradient / (jnp.sqrt(updated) + 1e-06), updated)

def reference(gradients, row_ids, hot_ids, embedding, moments, hot_table, hot_moments):
    ordered = jnp.sort(hot_ids)
    sorting = jnp.argsort(hot_ids).astype(jnp.int32)
    located = jnp.clip(jnp.searchsorted(ordered, row_ids), 0, HOT - 1).astype(jnp.int32)
    is_hot = ordered[located] == row_ids
    hot_index = sorting[located]
    values = gradients.astype(jnp.float32)
    hot_grad = jax.ops.segment_sum(jnp.where(is_hot[:, None], values, 0.0), hot_index, num_segments=HOT)
    cold_grad = jax.ops.segment_sum(jnp.where(is_hot[:, None], 0.0, values), row_ids, num_segments=ROWS)
    new_table, new_moments = adagrad(embedding, moments, cold_grad)
    new_hot_table, new_hot_moments = adagrad(hot_table, hot_moments, hot_grad)
    return (new_table, new_moments, new_hot_table, new_hot_moments)
```

```python
import functools

import jax
import jax.numpy as jnp
from jax import lax
from jax.experimental import pallas as pl
from jax.experimental.pallas import tpu as pltpu
from jax.sharding import Mesh
from jax.sharding import PartitionSpec as P

AXES = ("gx_0", "gx_1", "gy_0", "gy_1", "gz")
CAP = 4
ROWS = 256
BIG = 1.0e9
SUB = 4
MESH = pl.DeviceIdType.MESH
F32, BF16, I32 = jnp.float32, jnp.bfloat16, jnp.int32


def kernel(
    sizes, ids_ref, hot_ref, grad_ref, cold_ref, hotg_ref,
    mc, sb, rb, lt, lr, labs, dp, fw, bw, hs, hr, hp, hz, hq, hg, ho,
    ssem, rsem, lsem, zsend, fsem, bsem, hsem, sent,
):
    ny, nzh, nx, nc, nzl = sizes
    np_, nz = ny * nx * nc, nzh * nzl
    half = nz // 2
    tiles = ids_ref.shape[0]
    hot_rows = hs.shape[1]
    classes = hot_rows // 8
    y, zh, x, c, zl = (lax.axis_index(a) for a in AXES)
    me_p = (y * nx + x) * nc + c
    me_z = zh * nzl + zl

    def plane(p):
        return (p // (nx * nc), zh, (p // nc) % nx, p % nc, zl)

    def column(z):
        return (y, z // nzl, x, c, z % nzl)

    def mate(k):
        return lax.rem(me_p + k, np_)

    def above(k):
        return lax.rem(me_z + k, nz)

    def remote(src, dst, send, recv, device):
        return pltpu.make_async_remote_copy(
            src_ref=src, dst_ref=dst, send_sem=send, recv_sem=recv,
            device_id=device, device_id_type=MESH,
        )

    def whole(ref, sem):
        pltpu.make_async_copy(ref, ref, sem).wait()

    barrier = pltpu.get_barrier_semaphore()

    @pl.loop(1, np_)
    def _(k):
        pl.semaphore_signal(barrier, inc=1, device_id=plane(mate(k)), device_id_type=MESH)

    @pl.loop(1, nz)
    def _(k):
        pl.semaphore_signal(barrier, inc=1, device_id=column(above(k)), device_id_type=MESH)

    ids = [ids_ref[k : k + 1, :] for k in range(tiles)]
    idf = [v.astype(F32) for v in ids]
    grads = grad_ref[...]

    def match(i, found):
        row = hot_ref[pl.ds(i, 1), :].astype(F32)
        column_of = jnp.transpose(jnp.broadcast_to(row, (128, 128)))
        hits = [jnp.where(column_of == idf[k], 1.0, 0.0) for k in range(tiles)]
        sums = jnp.dot(
            jnp.concatenate(hits, axis=1).astype(BF16), grads, preferred_element_type=F32
        )
        parts = 128 // hot_rows
        hs[pl.ds(i * parts, parts)] = sums.reshape(parts, hot_rows, 128)
        return tuple(f + jnp.sum(h.reshape(16, 8, 128), axis=0) for f, h in zip(found, hits))

    none = tuple(jnp.zeros((8, 128), F32) for _ in range(tiles))
    found = lax.fori_loop(0, hot_ref.shape[0], match, none)

    owner = []
    for k in range(tiles):
        o = ids[k] // ROWS
        oz = (o // (nx * nc * nzl)) % nzh * nzl + o % nzl
        op = (o // (nx * nc * nzl * nzh) * nx + o // (nc * nzl) % nx) * nc + o // nzl % nc
        rel = (oz - me_z + nz) % nz
        step = jnp.where(rel == 0, 0, jnp.where(rel <= half, half - rel, rel - half))
        side = jnp.where((rel > half) | (rel == 0), 1, 0)
        place = (step * np_ + op) * 2 + side
        hot = jnp.sum(found[k], axis=0, keepdims=True) > 0.0
        owner.append(jnp.where(hot, -1, place))
    span = min(32, np_ * nz)

    def pick(b, carry):
        mine = lax.broadcasted_iota(I32, (span, 128), 0) + b * span
        left = [jnp.where(owner[k] == mine, idf[k], BIG) for k in range(tiles)]
        for j in range(CAP):
            low = left[0]
            for v in left[1:]:
                low = jnp.minimum(low, v)
            low = jnp.min(low, axis=1, keepdims=True)
            mc[pl.ds(b * span * CAP + j, span, stride=CAP), :] = jnp.broadcast_to(low, (span, 128))
            if j < CAP - 1:
                left = [jnp.where(v > low, v, BIG) for v in left]
        return carry

    lax.fori_loop(0, np_ * nz // span, pick, 0)

    group = np_ * 8
    lane = lax.broadcasted_iota(I32, (group, 128), 1)

    def label(s, total):
        low = mc[pl.ds(pl.multiple_of(s * group, group), group), :]
        value = jnp.where(low < BIG, (low.astype(I32) % ROWS + 1).astype(F32), 0.0)
        return jnp.where(lane == s, value, total)

    lt[...] = lax.fori_loop(0, half, label, jnp.zeros((group, 128), F32)).reshape(np_, 8, 128)

    pl.semaphore_wait(barrier, np_ - 1 + nz - 1)

    @pl.loop(1, np_)
    def _(k):
        p = mate(k)
        remote(lt.at[p], lr.at[me_p], sent.at[0], lsem, plane(p)).start()

    pltpu.make_async_copy(lt.at[me_p], lr.at[me_p], lsem).start()

    @pl.loop(0, half)
    def _(s):
        low = mc[pl.ds(pl.multiple_of(s * group, group), group), :]
        hits = [jnp.where(low == idf[k], 1.0, 0.0).astype(BF16) for k in range(tiles)]
        sums = jnp.dot(jnp.concatenate(hits, axis=1), grads, preferred_element_type=F32)
        sb[s] = sums.reshape(np_, 8, 128)

        @pl.loop(1, np_)
        def _(k):
            p = mate(k)
            remote(sb.at[s, p], rb.at[s, me_p], ssem.at[s], rsem.at[s], plane(p)).start()

        pltpu.make_async_copy(sb.at[s, me_p], rb.at[s, me_p], rsem.at[s]).start()

        @pl.when(s == 0)
        def _():
            @pl.loop(1, np_)
            def _(k):
                p = mate(k)
                remote(hs.at[p], hr.at[me_p], sent.at[1], hsem.at[0], plane(p)).start()

            pltpu.make_async_copy(hs.at[me_p], hr.at[me_p], hsem.at[0]).start()

    whole(lr, lsem)
    eye = lax.broadcasted_iota(I32, (8, 128), 0) == lax.broadcasted_iota(I32, (8, 128), 1)
    eye = jnp.where(eye, 1.0, 0.0).astype(BF16)
    rows = lax.dot_general(
        eye, lr[...].reshape(group, 128).astype(BF16), (((1,), (1,)), ((), ())),
        preferred_element_type=F32,
    )
    second = lax.broadcasted_iota(I32, (8, group), 1) % 8 >= CAP
    labs[...] = jnp.where(rows > 0.0, rows - 1.0 + jnp.where(second, float(ROWS), 0.0), -1.0)

    def dense(s):
        whole(rb.at[s], rsem.at[s])
        values = rb[s].reshape(group, 128)
        high = values.astype(BF16)
        low = (values - high.astype(F32)).astype(BF16)
        where = lax.broadcasted_iota(I32, (2 * ROWS, group), 0).astype(F32)
        spread = jnp.where(labs[pl.ds(s, 1), :] == where, 1.0, 0.0).astype(BF16)
        both = jnp.dot(spread, jnp.concatenate([high, low], axis=1), preferred_element_type=F32)
        dp[s] = both[:, :128] + both[:, 128:]

    piece = ROWS // SUB
    forward, back = column(above(1)), column(above(nz - 1))

    def ahead(t, j):
        part = pl.ds(j * piece, piece)
        return remote(dp.at[t, part], fw.at[t, part], zsend.at[0, t], fsem.at[t, j], forward)

    def behind(t, j, offset=ROWS):
        part = pl.ds(offset + j * piece, piece)
        land = bw.at[t, pl.ds(j * piece, piece)]
        return remote(dp.at[t, part], land, zsend.at[1, t], bsem.at[t, j], back)

    dense(0)
    for j in range(SUB // 2):
        ahead(0, j).start()
        behind(0, SUB // 2 + j, 0).start()
    dense(1)
    fw[0, ROWS // 2 :] = jnp.zeros((ROWS // 2, 128), F32)
    bw[0, : ROWS // 2] = jnp.zeros((ROWS // 2, 128), F32)

    whole(hr, hsem.at[0])

    def add_plane(k, total):
        return total + hr[k]

    total = lax.fori_loop(1, np_, add_plane, hr[0])
    hp[...] = total.reshape(classes, 8, 128)

    @pl.loop(1, nz)
    def _(k):
        z = above(k)
        remote(hp.at[z % classes], hz.at[me_z], sent.at[2], hsem.at[1], column(z)).start()

    pltpu.make_async_copy(hp.at[me_z % classes], hz.at[me_z], hsem.at[1]).start()
    family = me_z // classes * classes

    @pl.loop(1, half)
    def _(t):
        for j in range(SUB):
            part = pl.ds(j * piece, piece)
            other = pl.ds(ROWS + j * piece, piece)

            @pl.when((t > 1) | (j < SUB // 2))
            def _():
                pltpu.make_async_copy(fw.at[t - 1, part], fw.at[t - 1, part], fsem.at[t - 1, j]).wait()

            dp[t, part] += fw[t - 1, part]
            ahead(t, j).start()

            @pl.when((t > 1) | (j >= SUB // 2))
            def _():
                pltpu.make_async_copy(bw.at[t - 1, part], bw.at[t - 1, part], bsem.at[t - 1, j]).wait()

            dp[t, other] += bw[t - 1, part]
            behind(t, j).start()

        @pl.when(t == half // 2)
        def _():
            whole(hz, hsem.at[1])
            total = hz[0]
            for k in range(1, nz):
                total += hz[k]
            hq[...] = total
            for k in range(1, classes):
                z = family + lax.rem(me_z - family + k, classes)
                remote(hq, hg.at[me_z % classes], sent.at[3], hsem.at[2], column(z)).start()
            pltpu.make_async_copy(hq, hg.at[me_z % classes], hsem.at[2]).start()

        @pl.when(t == min(half // 2 + 1, half - 1))
        def _():
            whole(hg, hsem.at[2])

            @pl.loop(1, np_)
            def _(k):
                remote(hg, ho.at[me_p], sent.at[4], hsem.at[3], plane(mate(k))).start()

            pltpu.make_async_copy(hg, ho.at[me_p], hsem.at[3]).start()

        @pl.when(t + 1 < half)
        def _():
            dense(t + 1)

    last = half - 1
    for j in range(SUB):
        part = pl.ds(j * piece, piece)
        own = dp[0, pl.ds(ROWS + j * piece, piece)]
        pltpu.make_async_copy(fw.at[last, part], fw.at[last, part], fsem.at[last, j]).wait()
        pltpu.make_async_copy(bw.at[last, part], bw.at[last, part], bsem.at[last, j]).wait()
        cold_ref[part, :] = own + fw[last, part] + bw[last, part]
    whole(ho, hsem.at[3])
    hotg_ref[...] = ho[...].reshape(hotg_ref.shape)

    @pl.loop(0, half)
    def _(s):
        whole(sb.at[s, pl.ds(0, np_ - 1)], ssem.at[s])

    for d in range(2):
        whole(dp.at[0, pl.ds(0, ROWS // 2)], zsend.at[d, 0])

        @pl.loop(1, half)
        def _(t):
            whole(dp.at[t, pl.ds(0, ROWS)], zsend.at[d, t])

    whole(lt.at[pl.ds(0, np_ - 1)], sent.at[0])
    whole(hs.at[pl.ds(0, np_ - 1)], sent.at[1])
    whole(hz.at[pl.ds(0, nz - 1)], sent.at[2])
    whole(hg.at[pl.ds(0, classes - 1)], sent.at[3])
    whole(ho.at[pl.ds(0, np_ - 1)], sent.at[4])


def adagrad(weights, moments, gradient):
    updated = moments + gradient * gradient
    return (weights - 0.5 * gradient / (jnp.sqrt(updated) + 1e-06), updated)


def body(sizes, gradients, row_ids, hot_ids, embedding, moments, hot_table, hot_moments):
    ny, nzh, nx, nc, nzl = sizes
    np_, nz = ny * nx * nc, nzh * nzl
    half = nz // 2
    hot_rows = hot_ids.shape[0] // np_
    classes = hot_rows // 8
    width = gradients.shape[1]
    vmem = pl.BlockSpec(memory_space=pltpu.VMEM)
    dma = pltpu.SemaphoreType.DMA
    cold_grad, hot_grad = pl.pallas_call(
        functools.partial(kernel, sizes),
        out_shape=(
            jax.ShapeDtypeStruct((ROWS, width), F32),
            jax.ShapeDtypeStruct((hot_ids.shape[0], width), F32),
        ),
        in_specs=[vmem] * 3,
        out_specs=(vmem, vmem),
        scratch_shapes=[
            pltpu.VMEM((np_ * nz * CAP, 128), F32),
            pltpu.VMEM((half, np_, 8, 128), F32),
            pltpu.VMEM((half, np_, 8, 128), F32),
            pltpu.VMEM((np_, 8, 128), F32),
            pltpu.VMEM((np_, 8, 128), F32),
            pltpu.VMEM((8, np_ * 8), F32),
            pltpu.VMEM((half, 2 * ROWS, 128), F32),
            pltpu.VMEM((half, ROWS, 128), F32),
            pltpu.VMEM((half, ROWS, 128), F32),
            pltpu.VMEM((np_, hot_rows, 128), F32),
            pltpu.VMEM((np_, hot_rows, 128), F32),
            pltpu.VMEM((classes, 8, 128), F32),
            pltpu.VMEM((nz, 8, 128), F32),
            pltpu.VMEM((8, 128), F32),
            pltpu.VMEM((classes, 8, 128), F32),
            pltpu.VMEM((np_, classes, 8, 128), F32),
            dma((half,)),
            dma((half,)),
            dma,
            dma((2, half)),
            dma((half, SUB)),
            dma((half, SUB)),
            dma((4,)),
            dma((5,)),
        ],
        compiler_params=pltpu.CompilerParams(collective_id=0, has_side_effects=True),
    )(row_ids.reshape(-1, 128), hot_ids.reshape(-1, 128), gradients)
    new_table, new_moments = adagrad(embedding, moments, cold_grad)
    new_hot_table, new_hot_moments = adagrad(hot_table, hot_moments, hot_grad)
    return (new_table, new_moments, new_hot_table, new_hot_moments)


def program(torus):
    sizes = tuple(torus.shape[a] for a in AXES)
    rows = P(AXES, None)
    return jax.shard_map(
        functools.partial(body, sizes),
        mesh=torus,
        in_specs=(rows, P(AXES), P(), rows, rows, P(), P()),
        out_specs=(rows, rows, P(), P()),
        check_vma=False,
    )


def solution(mesh):
    shape = (mesh.shape["gx"] // 2, 2, mesh.shape["gy"] // 2, 2, mesh.shape["gz"])
    return program(Mesh(mesh.devices.reshape(shape), AXES))
```

```python
import functools

import jax
import jax.numpy as jnp
from jax import lax
from jax.experimental import pallas as pl
from jax.experimental.pallas import tpu as pltpu
from jax.sharding import Mesh
from jax.sharding import PartitionSpec as P

AXES = ("gx_0", "gx_1", "gy_0", "gy_1", "gz")
CAP = 4
ROWS = 256
BIG = 1.0e9
SUB = 4
MESH = pl.DeviceIdType.MESH
F32, BF16, I32 = jnp.float32, jnp.bfloat16, jnp.int32


def half_of(n):
    return n.bit_length() - 1


def over(v, n):
    return v >> half_of(n)


def under(v, n):
    return v & (n - 1)


NEAR = ((8, 7), (6, 5), (-7, -6), (4, -5), (3, -4), (2, -3), (1, -2), (0, -1))
SHIFT = (3, 1, -2)
FAR = len(SHIFT)
STEPS = 5


def kernel(
    sizes, ids_ref, hot_ref, grad_ref, cold_ref, hotg_ref,
    hc, mc, sb, rb, lt, lr, labs, dp, fw, bw, hs, hr, hp, hz, hq, hg, ho,
    ssem, rsem, lsend, lsem, zsend, fsem, bsem, hsem, sent,
):
    ny, nzh, nx, nc, nzl = sizes
    np_, nz = ny * nx * nc, nzh * nzl
    tiles = ids_ref.shape[0]
    hot_rows = hs.shape[1]
    classes = hot_rows // 8
    group = np_ * 8
    y, zh, x, c, zl = (lax.axis_index(a) for a in AXES)
    me_p = (y * nx + x) * nc + c
    me_z = zh * nzl + zl
    sign = 1 - 2 * c

    def at(p, z):
        return (over(p, nx * nc), over(z, nzl), under(over(p, nc), nx), under(p, nc), under(z, nzl))

    def plane(p):
        return at(p, me_z)

    def column(z):
        return at(me_p, z)

    def mate(k):
        return under(me_p + k, np_)

    def above(k):
        return under(me_z + nz + k, nz)

    def remote(src, dst, send, recv, device):
        return pltpu.make_async_remote_copy(
            src_ref=src, dst_ref=dst, send_sem=send, recv_sem=recv,
            device_id=device, device_id_type=MESH,
        )

    def whole(ref, sem):
        pltpu.make_async_copy(ref, ref, sem).wait()

    barrier = pltpu.get_barrier_semaphore()

    def greet(device):
        pl.semaphore_signal(barrier, inc=1, device_id=device, device_id_type=MESH)

    for shift in SHIFT:

        @pl.loop(0, np_)
        def _(k):
            greet(at(mate(k), above(-sign * shift)))

    @pl.loop(1, np_)
    def _(k):
        greet(plane(mate(k)))

    @pl.loop(1, nz)
    def _(k):
        greet(column(above(k)))

    idf = [ids_ref[k : k + 1, :].astype(F32) for k in range(tiles)]
    found = [jnp.zeros((8, 128), F32) for _ in range(tiles)]
    for i in range(hot_ref.shape[0]):
        row = hot_ref[i : i + 1, :].astype(F32)
        column_of = jnp.transpose(jnp.broadcast_to(row, (128, 128)))
        hc[i * 128 : (i + 1) * 128, :] = column_of
        for r in range(16):
            part = column_of[r * 8 : r * 8 + 8]
            found = [jnp.where(part == idf[k], 1.0, found[k]) for k in range(tiles)]

    cold = [
        jnp.where(jnp.max(found[k], axis=0, keepdims=True) > 0.0, -1.0, idf[k])
        for k in range(tiles)
    ]
    pair = lax.broadcasted_iota(I32, (np_ * 2, 128), 0)
    col = over(pair, 2)
    turn = 1 - 2 * under(col, nc)
    floors = []
    for near in NEAR:
        z = under(me_z + nz + turn * jnp.where(under(pair, 2) == 0, *near), nz)
        o = (over(col, nx * nc) * nzh + over(z, nzl)) * nx + under(over(col, nc), nx)
        o = (o * nc + under(col, nc)) * nzl + under(z, nzl)
        floors.append((o * ROWS).astype(F32))
    lows = [f - 1.0 for f in floors]
    for j in range(CAP):
        for s in range(len(NEAR)):
            low = jnp.where(cold[0] > lows[s], cold[0], BIG)
            for k in range(1, tiles):
                low = jnp.minimum(low, jnp.where(cold[k] > lows[s], cold[k], BIG))
            low = jnp.broadcast_to(jnp.min(low, axis=1, keepdims=True), pair.shape)
            lows[s] = jnp.where(low < floors[s] + float(ROWS), low, BIG)
            mc[pl.ds(s * group + j, np_ * 2, stride=CAP), :] = lows[s]

    lane = lax.broadcasted_iota(I32, (group, 128), 1)
    slot = under(lax.broadcasted_iota(I32, (group, 128), 0), 8)
    total = jnp.zeros((group, 128), F32)
    for s in range(len(NEAR)):
        low = mc[s * group : (s + 1) * group, :]
        value = jnp.where(low < BIG, under(low.astype(I32), ROWS).astype(F32) + 1.0, 0.0)
        total = jnp.where(lane == s * 8 + slot, value, total)
    lt[...] = jnp.sum(total.reshape(np_, 8, 128), axis=1, keepdims=True)

    pl.semaphore_wait(barrier, FAR * np_ + np_ - 1 + nz - 1)

    def target(s, p):
        return at(p, above((1 - 2 * under(p, nc)) * SHIFT[s]))

    for s in range(FAR):

        @pl.loop(0, np_)
        def _(k):
            p = mate(k)
            remote(lt.at[p], lr.at[s, me_p], lsend.at[s], lsem.at[s], target(s, p)).start()

    @pl.loop(1, np_)
    def _(k):
        p = mate(k)
        remote(lt.at[p], lr.at[FAR, me_p], lsend.at[FAR], lsem.at[FAR], plane(p)).start()

    pltpu.make_async_copy(lt.at[me_p], lr.at[FAR, me_p], lsem.at[FAR]).start()

    grads = grad_ref[...]

    def slots(s):
        low = mc[pl.ds(pl.multiple_of(s * group, group), group), :]
        hits = [jnp.where(low == idf[k], 1.0, 0.0).astype(BF16) for k in range(tiles)]
        sums = jnp.dot(jnp.concatenate(hits, axis=1), grads, preferred_element_type=F32)
        sb[s] = sums.reshape(np_, 8, 128)

    def share(s):
        slots(s)

        @pl.loop(1, np_)
        def _(k):
            p = mate(k)
            remote(sb.at[s, p], rb.at[s, me_p], ssem.at[s], rsem.at[s], plane(p)).start()

        pltpu.make_async_copy(sb.at[s, me_p], rb.at[s, me_p], rsem.at[s]).start()

    for s in (0, 2, 1):
        slots(s)

        @pl.loop(0, np_)
        def _(k):
            p = mate(k)
            remote(sb.at[s, p], rb.at[s, me_p], ssem.at[s], rsem.at[s], target(s, p)).start()

    share(FAR)

    @pl.loop(0, hs.shape[0] * hot_rows // 128)
    def _(i):
        part = hc[pl.ds(pl.multiple_of(i * 128, 128), 128), :]
        hits = [jnp.where(part == idf[k], 1.0, 0.0).astype(BF16) for k in range(tiles)]
        sums = jnp.dot(jnp.concatenate(hits, axis=1), grads, preferred_element_type=F32)
        parts = 128 // hot_rows
        hs[pl.ds(i * parts, parts)] = sums.reshape(parts, hot_rows, 128)

    @pl.loop(1, np_)
    def _(k):
        p = mate(k)
        remote(hs.at[p], hr.at[me_p], sent.at[1], hsem.at[0], plane(p)).start()

    pltpu.make_async_copy(hs.at[me_p], hr.at[me_p], hsem.at[0]).start()

    @pl.loop(FAR + 1, len(NEAR))
    def _(s):
        share(s)

    for s in range(FAR + 1):
        whole(lr.at[s], lsem.at[s])
    lane = lax.broadcasted_iota(I32, (np_, 128), 1)
    known = lr[FAR].reshape(np_, 128)
    for s in range(FAR):
        known = jnp.where(over(lane, 8) == s, lr[s].reshape(np_, 128), known)
    spread = over(lax.broadcasted_iota(I32, (group, np_), 0), 8)
    spread = spread == lax.broadcasted_iota(I32, (group, np_), 1)
    wide = jnp.dot(
        jnp.where(spread, 1.0, 0.0).astype(BF16), known.astype(BF16), preferred_element_type=F32
    )
    lane = lax.broadcasted_iota(I32, (group, 128), 1)
    wide = jnp.where(under(lane, 8) == slot, wide, 0.0).astype(BF16)
    tile = over(lax.broadcasted_iota(I32, (8, 128), 1), 8)
    tile = tile == lax.broadcasted_iota(I32, (8, 128), 0)
    rows = lax.dot_general(
        jnp.where(tile, 1.0, 0.0).astype(BF16), wide, (((1,), (1,)), ((), ())),
        preferred_element_type=F32,
    )
    second = under(lax.broadcasted_iota(I32, (8, group), 1), 8) >= CAP
    labs[...] = jnp.where(rows > 0.0, rows - 1.0 + jnp.where(second, float(ROWS), 0.0), -1.0)

    def dense(s):
        whole(rb.at[s], rsem.at[s])
        values = rb[s].reshape(group, 128)
        high = values.astype(BF16)
        low = (values - high.astype(F32)).astype(BF16)
        where = lax.broadcasted_iota(I32, (2 * ROWS, group), 0).astype(F32)
        spread = jnp.where(labs[pl.ds(s, 1), :] == where, 1.0, 0.0).astype(BF16)
        both = jnp.dot(spread, jnp.concatenate([high, low], axis=1), preferred_element_type=F32)
        both = both[:, :128] + both[:, 128:]
        return both[:ROWS], both[ROWS:]

    piece = ROWS // SUB
    front, rear = column(above(sign)), column(above(-sign))
    main, side = pl.ds(0, ROWS), pl.ds(ROWS, ROWS)

    def send(i, j):
        part = pl.ds(j * piece, piece)
        other = pl.ds(ROWS + j * piece, piece)
        return (
            remote(dp.at[i, part], fw.at[i, part], zsend.at[0, i], fsem.at[i, j], front),
            remote(dp.at[i, other], bw.at[i, part], zsend.at[1, i], bsem.at[i, j], rear),
        )

    dp[0, main], dp[1, main] = dense(0)
    dp[0, side], dp[1, side] = dense(2)
    first, second = dense(1)
    dp[0, main] += first
    dp[1, main] += second
    first, second = dense(3)
    dp[1, main] += first
    dp[0, side] += second
    for j in range(SUB):
        for copy in send(0, j):
            copy.start()
    for i in range(2, STEPS):
        dp[i, side] = jnp.zeros((ROWS, 128), F32)
    dp[2, main], second = dense(4)
    dp[1, side] += second

    whole(hr, hsem.at[0])

    def add_plane(k, total):
        return total + hr[k]

    total = lax.fori_loop(1, np_, add_plane, hr[0])
    hp[...] = total.reshape(classes, 8, 128)

    @pl.loop(1, nz)
    def _(k):
        z = above(k)
        remote(hp.at[under(z, classes)], hz.at[me_z], sent.at[2], hsem.at[1], column(z)).start()

    pltpu.make_async_copy(hp.at[under(me_z, classes)], hz.at[me_z], hsem.at[1]).start()
    family = me_z - under(me_z, classes)

    @pl.loop(1, STEPS)
    def _(i):
        for j in range(SUB):
            part = pl.ds(j * piece, piece)
            other = pl.ds(ROWS + j * piece, piece)
            ahead, behind = send(i, j)
            whole(fw.at[i - 1, part], fsem.at[i - 1, j])
            dp[i, part] += fw[i - 1, part]
            ahead.start()
            whole(bw.at[i - 1, part], bsem.at[i - 1, j])
            dp[i, other] += bw[i - 1, part]
            behind.start()

        @pl.when(i == 2)
        def _():
            whole(hz, hsem.at[1])
            total = hz[0]
            for k in range(1, nz):
                total += hz[k]
            hq[...] = total
            for k in range(1, classes):
                z = family + under(me_z + k, classes)
                here = hg.at[under(me_z, classes)]
                remote(hq, here, sent.at[3], hsem.at[2], column(z)).start()
            pltpu.make_async_copy(hq, hg.at[under(me_z, classes)], hsem.at[2]).start()

        @pl.when(i == 3)
        def _():
            whole(hg, hsem.at[2])

            @pl.loop(1, np_)
            def _(k):
                remote(hg, ho.at[me_p], sent.at[4], hsem.at[3], plane(mate(k))).start()

            pltpu.make_async_copy(hg, ho.at[me_p], hsem.at[3]).start()

        @pl.when(i + 4 < len(NEAR))
        def _():
            first, second = dense(i + 4)
            dp[i + 2, main] = first
            dp[i + 1, side] += second

    last = STEPS - 1
    for j in range(SUB):
        part = pl.ds(j * piece, piece)
        whole(fw.at[last, part], fsem.at[last, j])
        whole(bw.at[last, part], bsem.at[last, j])
        cold_ref[part, :] = dp[STEPS, part] + fw[last, part] + bw[last, part]
    whole(ho, hsem.at[3])
    hotg_ref[...] = ho[...].reshape(hotg_ref.shape)

    for s in range(FAR):
        whole(sb.at[s], ssem.at[s])
        whole(lt, lsend.at[s])
    whole(lt.at[pl.ds(0, np_ - 1)], lsend.at[FAR])

    @pl.loop(FAR, len(NEAR))
    def _(s):
        whole(sb.at[s, pl.ds(0, np_ - 1)], ssem.at[s])

    @pl.loop(0, STEPS)
    def _(i):
        whole(fw.at[i], zsend.at[0, i])
        whole(bw.at[i], zsend.at[1, i])

    whole(hs.at[pl.ds(0, np_ - 1)], sent.at[1])
    whole(hz.at[pl.ds(0, nz - 1)], sent.at[2])
    whole(hg.at[pl.ds(0, classes - 1)], sent.at[3])
    whole(ho.at[pl.ds(0, np_ - 1)], sent.at[4])


def adagrad(weights, moments, gradient):
    updated = moments + gradient * gradient
    return (weights - 0.5 * gradient / (jnp.sqrt(updated) + 1e-06), updated)


def body(sizes, gradients, row_ids, hot_ids, embedding, moments, hot_table, hot_moments):
    ny, nzh, nx, nc, nzl = sizes
    np_, nz = ny * nx * nc, nzh * nzl
    tiles = len(NEAR)
    hot_rows = hot_ids.shape[0] // np_
    classes = hot_rows // 8
    width = gradients.shape[1]
    vmem = pl.BlockSpec(memory_space=pltpu.VMEM)
    dma = pltpu.SemaphoreType.DMA
    cold_grad, hot_grad = pl.pallas_call(
        functools.partial(kernel, sizes),
        out_shape=(
            jax.ShapeDtypeStruct((ROWS, width), F32),
            jax.ShapeDtypeStruct((hot_ids.shape[0], width), F32),
        ),
        in_specs=[vmem] * 3,
        out_specs=(vmem, vmem),
        scratch_shapes=[
            pltpu.VMEM((hot_ids.shape[0], 128), F32),
            pltpu.VMEM((tiles * np_ * 8, 128), F32),
            pltpu.VMEM((tiles, np_, 8, 128), F32),
            pltpu.VMEM((tiles, np_, 8, 128), F32),
            pltpu.VMEM((np_, 1, 128), F32),
            pltpu.VMEM((FAR + 1, np_, 1, 128), F32),
            pltpu.VMEM((8, np_ * 8), F32),
            pltpu.VMEM((STEPS + 1, 2 * ROWS, 128), F32),
            pltpu.VMEM((STEPS, ROWS, 128), F32),
            pltpu.VMEM((STEPS, ROWS, 128), F32),
            pltpu.VMEM((np_, hot_rows, 128), F32),
            pltpu.VMEM((np_, hot_rows, 128), F32),
            pltpu.VMEM((classes, 8, 128), F32),
            pltpu.VMEM((nz, 8, 128), F32),
            pltpu.VMEM((8, 128), F32),
            pltpu.VMEM((classes, 8, 128), F32),
            pltpu.VMEM((np_, classes, 8, 128), F32),
            dma((tiles,)),
            dma((tiles,)),
            dma((FAR + 1,)),
            dma((FAR + 1,)),
            dma((2, STEPS)),
            dma((STEPS, SUB)),
            dma((STEPS, SUB)),
            dma((4,)),
            dma((5,)),
        ],
        compiler_params=pltpu.CompilerParams(collective_id=0, has_side_effects=True),
    )(row_ids.reshape(-1, 128), hot_ids.reshape(-1, 128), gradients)
    new_table, new_moments = adagrad(embedding, moments, cold_grad)
    new_hot_table, new_hot_moments = adagrad(hot_table, hot_moments, hot_grad)
    return (new_table, new_moments, new_hot_table, new_hot_moments)


def program(torus):
    sizes = tuple(torus.shape[a] for a in AXES)
    rows = P(AXES, None)
    return jax.shard_map(
        functools.partial(body, sizes),
        mesh=torus,
        in_specs=(rows, P(AXES), P(), rows, rows, P(), P()),
        out_specs=(rows, rows, P(), P()),
        check_vma=False,
    )


def solution(mesh):
    shape = (mesh.shape["gx"] // 2, 2, mesh.shape["gy"] // 2, 2, mesh.shape["gz"])
    return program(Mesh(mesh.devices.reshape(shape), AXES))
```

```python
import functools

import jax
import jax.numpy as jnp
from jax import lax
from jax.experimental import pallas as pl
from jax.experimental.pallas import tpu as pltpu
from jax.sharding import Mesh
from jax.sharding import PartitionSpec as P

AXES = ("gx_0", "gx_1", "gy_0", "gy_1", "gz")
CAP = 4
ROWS = 256
BIG = 1.0e9
SUB = 4
MESH = pl.DeviceIdType.MESH
F32, BF16, I32 = jnp.float32, jnp.bfloat16, jnp.int32


def half_of(n):
    return n.bit_length() - 1


def over(v, n):
    return v >> half_of(n)


def under(v, n):
    return v & (n - 1)


NEAR = ((8, 7), (6, -7), (5, -6), (4, -5), (3, -4), (2, -3), (1, -2), (0, -1))
SHIFT = (1,)
FAR = len(SHIFT)
STEPS = 7
HOT_IN, HOT_SUM, HOT_OUT = 1, 3, 5


def kernel(
    sizes, ids_ref, hot_ref, grad_ref, cold_ref, hotg_ref,
    hc, mc, sb, rb, lt, lr, labs, dp, fw, bw, hs, hr, hp, hz, hq, hg, ho,
    ssem, rsem, lsend, lsem, zsend, fsem, bsem, hsem, sent, relay,
):
    ny, nzh, nx, nc, nzl = sizes
    np_, nz = ny * nx * nc, nzh * nzl
    tiles = ids_ref.shape[0]
    hot_rows = hs.shape[1]
    classes = hot_rows // 8
    group = np_ * 8
    y, zh, x, c, zl = (lax.axis_index(a) for a in AXES)
    me_p = (y * nx + x) * nc + c
    me_z = zh * nzl + zl
    sign = 1 - 2 * c

    def at(p, z):
        return (over(p, nx * nc), over(z, nzl), under(over(p, nc), nx), under(p, nc), under(z, nzl))

    def plane(p):
        return at(p, me_z)

    def column(z):
        return at(me_p, z)

    def mate(k):
        return under(me_p + k, np_)

    def above(k):
        return under(me_z + nz + k, nz)

    def remote(src, dst, send, recv, device):
        return pltpu.make_async_remote_copy(
            src_ref=src, dst_ref=dst, send_sem=send, recv_sem=recv,
            device_id=device, device_id_type=MESH,
        )

    def whole(ref, sem):
        pltpu.make_async_copy(ref, ref, sem).wait()

    barrier = pltpu.get_barrier_semaphore()

    def greet(sem, device):
        pl.semaphore_signal(sem, inc=1, device_id=device, device_id_type=MESH)

    greet(barrier, column(above(1)))
    greet(barrier, column(above(-1)))

    @pl.loop(1, np_)
    def _(k):
        greet(barrier, plane(mate(k)))

    def pass_on(r):
        greet(relay.at[r], column(above(2**r)))
        greet(relay.at[r], column(above(-(2**r))))

    idf = [ids_ref[k : k + 1, :].astype(F32) for k in range(tiles)]
    found = [jnp.zeros((8, 128), F32) for _ in range(tiles)]
    for i in range(hot_ref.shape[0]):
        row = hot_ref[i : i + 1, :].astype(F32)
        column_of = jnp.transpose(jnp.broadcast_to(row, (128, 128)))
        hc[i * 128 : (i + 1) * 128, :] = column_of
        for r in range(16):
            part = column_of[r * 8 : r * 8 + 8]
            found = [jnp.where(part == idf[k], 1.0, found[k]) for k in range(tiles)]

    cold = [
        jnp.where(jnp.max(found[k], axis=0, keepdims=True) > 0.0, -1.0, idf[k])
        for k in range(tiles)
    ]
    pair = lax.broadcasted_iota(I32, (np_ * 2, 128), 0)
    col = over(pair, 2)
    turn = 1 - 2 * under(col, nc)
    floors = []
    for near in NEAR:
        z = under(me_z + nz + turn * jnp.where(under(pair, 2) == 0, *near), nz)
        o = (over(col, nx * nc) * nzh + over(z, nzl)) * nx + under(over(col, nc), nx)
        o = (o * nc + under(col, nc)) * nzl + under(z, nzl)
        floors.append((o * ROWS).astype(F32))
    lows = [f - 1.0 for f in floors]
    for j in range(CAP):
        for s in range(len(NEAR)):
            low = jnp.where(cold[0] > lows[s], cold[0], BIG)
            for k in range(1, tiles):
                low = jnp.minimum(low, jnp.where(cold[k] > lows[s], cold[k], BIG))
            low = jnp.broadcast_to(jnp.min(low, axis=1, keepdims=True), pair.shape)
            lows[s] = jnp.where(low < floors[s] + float(ROWS), low, BIG)
            mc[pl.ds(s * group + j, np_ * 2, stride=CAP), :] = lows[s]

    lane = lax.broadcasted_iota(I32, (group, 128), 1)
    slot = under(lax.broadcasted_iota(I32, (group, 128), 0), 8)
    total = jnp.zeros((group, 128), F32)
    for s in range(len(NEAR)):
        low = mc[s * group : (s + 1) * group, :]
        value = jnp.where(low < BIG, under(low.astype(I32), ROWS).astype(F32) + 1.0, 0.0)
        total = jnp.where(lane == s * 8 + slot, value, total)
    lt[...] = jnp.sum(total.reshape(np_, 8, 128), axis=1, keepdims=True)

    grads = grad_ref[...]

    def slots(s):
        low = mc[pl.ds(pl.multiple_of(s * group, group), group), :]
        hits = [jnp.where(low == idf[k], 1.0, 0.0).astype(BF16) for k in range(tiles)]
        sums = jnp.dot(jnp.concatenate(hits, axis=1), grads, preferred_element_type=F32)
        sb[s] = sums.reshape(np_, 8, 128)

    for s in range(FAR + 1):
        slots(s)

    @pl.loop(0, hs.shape[0] * hot_rows // 128)
    def _(i):
        part = hc[pl.ds(pl.multiple_of(i * 128, 128), 128), :]
        hits = [jnp.where(part == idf[k], 1.0, 0.0).astype(BF16) for k in range(tiles)]
        sums = jnp.dot(jnp.concatenate(hits, axis=1), grads, preferred_element_type=F32)
        parts = 128 // hot_rows
        hs[pl.ds(i * parts, parts)] = sums.reshape(parts, hot_rows, 128)

    pl.semaphore_wait(barrier, 2 + np_ - 1)
    pass_on(0)

    def share(src, dst, send, recv):
        @pl.loop(1, np_)
        def _(k):
            p = mate(k)
            remote(src.at[p], dst.at[me_p], send, recv, plane(p)).start()

        pltpu.make_async_copy(src.at[me_p], dst.at[me_p], recv).start()

    def share_far(src, dst, send, recv, shift):
        @pl.loop(0, np_)
        def _(k):
            p = mate(k)
            z = above((1 - 2 * under(p, nc)) * shift)
            remote(src.at[p], dst.at[me_p], send, recv, at(p, z)).start()

    share(lt, lr.at[FAR], lsend.at[FAR], lsem.at[FAR])
    share(sb.at[FAR], rb.at[FAR], ssem.at[FAR], rsem.at[FAR])
    pl.semaphore_wait(relay.at[0], 2)
    pass_on(1)
    for s in range(FAR):
        share_far(lt, lr.at[s], lsend.at[s], lsem.at[s], SHIFT[s])
        share_far(sb.at[s], rb.at[s], ssem.at[s], rsem.at[s], SHIFT[s])

    def near(s):
        slots(s)
        share(sb.at[s], rb.at[s], ssem.at[s], rsem.at[s])

    near(FAR + 1)
    share(hs, hr, sent.at[1], hsem.at[0])
    pl.semaphore_wait(relay.at[1], 2)
    pass_on(2)

    @pl.loop(FAR + 2, len(NEAR))
    def _(s):
        near(s)

    for s in range(FAR + 1):
        whole(lr.at[s], lsem.at[s])
    lane = lax.broadcasted_iota(I32, (np_, 128), 1)
    known = lr[FAR].reshape(np_, 128)
    for s in range(FAR):
        known = jnp.where(over(lane, 8) == s, lr[s].reshape(np_, 128), known)
    spread = over(lax.broadcasted_iota(I32, (group, np_), 0), 8)
    spread = spread == lax.broadcasted_iota(I32, (group, np_), 1)
    wide = jnp.dot(
        jnp.where(spread, 1.0, 0.0).astype(BF16), known.astype(BF16), preferred_element_type=F32
    )
    lane = lax.broadcasted_iota(I32, (group, 128), 1)
    wide = jnp.where(under(lane, 8) == slot, wide, 0.0).astype(BF16)
    tile = over(lax.broadcasted_iota(I32, (8, 128), 1), 8)
    tile = tile == lax.broadcasted_iota(I32, (8, 128), 0)
    rows = lax.dot_general(
        jnp.where(tile, 1.0, 0.0).astype(BF16), wide, (((1,), (1,)), ((), ())),
        preferred_element_type=F32,
    )
    second = under(lax.broadcasted_iota(I32, (8, group), 1), 8) >= CAP
    labs[...] = jnp.where(rows > 0.0, rows - 1.0 + jnp.where(second, float(ROWS), 0.0), -1.0)

    def dense(s):
        whole(rb.at[s], rsem.at[s])
        values = rb[s].reshape(group, 128)
        high = values.astype(BF16)
        low = (values - high.astype(F32)).astype(BF16)
        where = lax.broadcasted_iota(I32, (2 * ROWS, group), 0).astype(F32)
        spread = jnp.where(labs[pl.ds(s, 1), :] == where, 1.0, 0.0).astype(BF16)
        both = jnp.dot(spread, jnp.concatenate([high, low], axis=1), preferred_element_type=F32)
        both = both[:, :128] + both[:, 128:]
        return both[:ROWS], both[ROWS:]

    piece = ROWS // SUB
    front, rear = column(above(sign)), column(above(-sign))
    main, side = pl.ds(0, ROWS), pl.ds(ROWS, ROWS)

    def send(i, j):
        part = pl.ds(j * piece, piece)
        other = pl.ds(ROWS + j * piece, piece)
        return (
            remote(dp.at[i, part], fw.at[i, part], zsend.at[0, i], fsem.at[i, j], front),
            remote(dp.at[i, other], bw.at[i, part], zsend.at[1, i], bsem.at[i, j], rear),
        )

    dp[0, main], dp[1, main] = dense(0)
    first, second = dense(1)
    dp[1, main] += first
    dp[0, side] = second
    for j in range(SUB):
        for copy in send(0, j):
            copy.start()
    dp[2, main], dp[1, side] = dense(2)

    family = me_z - under(me_z, classes)

    @pl.loop(1, STEPS)
    def _(i):
        for j in range(SUB):
            part = pl.ds(j * piece, piece)
            other = pl.ds(ROWS + j * piece, piece)
            ahead, behind = send(i, j)
            whole(fw.at[i - 1, part], fsem.at[i - 1, j])
            dp[i, part] += fw[i - 1, part]
            ahead.start()
            whole(bw.at[i - 1, part], bsem.at[i - 1, j])
            dp[i, other] += bw[i - 1, part]
            behind.start()

        @pl.when(i == HOT_IN)
        def _():
            whole(hr, hsem.at[0])

            def add_plane(k, total):
                return total + hr[k]

            total = lax.fori_loop(1, np_, add_plane, hr[0])
            hp[...] = total.reshape(classes, 8, 128)

            pl.semaphore_wait(relay.at[2], 2)

            @pl.loop(1, nz)
            def _(k):
                z = above(k)
                remote(hp.at[under(z, classes)], hz.at[me_z], sent.at[2], hsem.at[1], column(z)).start()

            pltpu.make_async_copy(hp.at[under(me_z, classes)], hz.at[me_z], hsem.at[1]).start()

        @pl.when(i == HOT_SUM)
        def _():
            whole(hz, hsem.at[1])
            total = hz[0]
            for k in range(1, nz):
                total += hz[k]
            hq[...] = total
            for k in range(1, classes):
                z = family + under(me_z + k, classes)
                here = hg.at[under(me_z, classes)]
                remote(hq, here, sent.at[3], hsem.at[2], column(z)).start()
            pltpu.make_async_copy(hq, hg.at[under(me_z, classes)], hsem.at[2]).start()

        @pl.when(i == HOT_OUT)
        def _():
            whole(hg, hsem.at[2])

            @pl.loop(1, np_)
            def _(k):
                remote(hg, ho.at[me_p], sent.at[4], hsem.at[3], plane(mate(k))).start()

            pltpu.make_async_copy(hg, ho.at[me_p], hsem.at[3]).start()

        @pl.when(i + 2 < len(NEAR))
        def _():
            dp[i + 2, main], dp[i + 1, side] = dense(i + 2)

    last = STEPS - 1
    for j in range(SUB):
        part = pl.ds(j * piece, piece)
        whole(fw.at[last, part], fsem.at[last, j])
        whole(bw.at[last, part], bsem.at[last, j])
        cold_ref[part, :] = dp[STEPS, part] + fw[last, part] + bw[last, part]
    whole(ho, hsem.at[3])
    hotg_ref[...] = ho[...].reshape(hotg_ref.shape)

    for s in range(FAR):
        whole(sb.at[s], ssem.at[s])
        whole(lt, lsend.at[s])
    whole(lt.at[pl.ds(0, np_ - 1)], lsend.at[FAR])

    @pl.loop(FAR, len(NEAR))
    def _(s):
        whole(sb.at[s, pl.ds(0, np_ - 1)], ssem.at[s])

    @pl.loop(0, STEPS)
    def _(i):
        whole(fw.at[i], zsend.at[0, i])
        whole(bw.at[i], zsend.at[1, i])

    whole(hs.at[pl.ds(0, np_ - 1)], sent.at[1])
    whole(hz.at[pl.ds(0, nz - 1)], sent.at[2])
    whole(hg.at[pl.ds(0, classes - 1)], sent.at[3])
    whole(ho.at[pl.ds(0, np_ - 1)], sent.at[4])


def adagrad(weights, moments, gradient):
    updated = moments + gradient * gradient
    return (weights - 0.5 * gradient / (jnp.sqrt(updated) + 1e-06), updated)


def body(sizes, gradients, row_ids, hot_ids, embedding, moments, hot_table, hot_moments):
    ny, nzh, nx, nc, nzl = sizes
    np_, nz = ny * nx * nc, nzh * nzl
    tiles = len(NEAR)
    hot_rows = hot_ids.shape[0] // np_
    classes = hot_rows // 8
    width = gradients.shape[1]
    vmem = pl.BlockSpec(memory_space=pltpu.VMEM)
    dma = pltpu.SemaphoreType.DMA
    cold_grad, hot_grad = pl.pallas_call(
        functools.partial(kernel, sizes),
        out_shape=(
            jax.ShapeDtypeStruct((ROWS, width), F32),
            jax.ShapeDtypeStruct((hot_ids.shape[0], width), F32),
        ),
        in_specs=[vmem] * 3,
        out_specs=(vmem, vmem),
        scratch_shapes=[
            pltpu.VMEM((hot_ids.shape[0], 128), F32),
            pltpu.VMEM((tiles * np_ * 8, 128), F32),
            pltpu.VMEM((tiles, np_, 8, 128), F32),
            pltpu.VMEM((tiles, np_, 8, 128), F32),
            pltpu.VMEM((np_, 1, 128), F32),
            pltpu.VMEM((FAR + 1, np_, 1, 128), F32),
            pltpu.VMEM((8, np_ * 8), F32),
            pltpu.VMEM((STEPS + 1, 2 * ROWS, 128), F32),
            pltpu.VMEM((STEPS, ROWS, 128), F32),
            pltpu.VMEM((STEPS, ROWS, 128), F32),
            pltpu.VMEM((np_, hot_rows, 128), F32),
            pltpu.VMEM((np_, hot_rows, 128), F32),
            pltpu.VMEM((classes, 8, 128), F32),
            pltpu.VMEM((nz, 8, 128), F32),
            pltpu.VMEM((8, 128), F32),
            pltpu.VMEM((classes, 8, 128), F32),
            pltpu.VMEM((np_, classes, 8, 128), F32),
            dma((tiles,)),
            dma((tiles,)),
            dma((FAR + 1,)),
            dma((FAR + 1,)),
            dma((2, STEPS)),
            dma((STEPS, SUB)),
            dma((STEPS, SUB)),
            dma((4,)),
            dma((5,)),
            pltpu.SemaphoreType.REGULAR((3,)),
        ],
        compiler_params=pltpu.CompilerParams(collective_id=0, has_side_effects=True),
    )(row_ids.reshape(-1, 128), hot_ids.reshape(-1, 128), gradients)
    new_table, new_moments = adagrad(embedding, moments, cold_grad)
    new_hot_table, new_hot_moments = adagrad(hot_table, hot_moments, hot_grad)
    return (new_table, new_moments, new_hot_table, new_hot_moments)


def program(torus):
    sizes = tuple(torus.shape[a] for a in AXES)
    rows = P(AXES, None)
    return jax.shard_map(
        functools.partial(body, sizes),
        mesh=torus,
        in_specs=(rows, P(AXES), P(), rows, rows, P(), P()),
        out_specs=(rows, rows, P(), P()),
        check_vma=False,
    )


def solution(mesh):
    shape = (mesh.shape["gx"] // 2, 2, mesh.shape["gy"] // 2, 2, mesh.shape["gz"])
    return program(Mesh(mesh.devices.reshape(shape), AXES))
```

```python
import functools

import jax
import jax.numpy as jnp
from jax import lax
from jax.experimental import pallas as pl
from jax.experimental.pallas import tpu as pltpu
from jax.sharding import Mesh
from jax.sharding import PartitionSpec as P

AXES = ("gx_0", "gx_1", "gy_0", "gy_1", "gz")
CAP = 4
ROWS = 256
BIG = 1.0e9
SUB = 4
MESH = pl.DeviceIdType.MESH
F32, BF16, I32 = jnp.float32, jnp.bfloat16, jnp.int32


def half_of(n):
    return n.bit_length() - 1


def over(v, n):
    return v >> half_of(n)


def under(v, n):
    return v & (n - 1)


NEAR = ((8, 7), (6, -7), (5, -6), (4, -5), (3, -4), (2, -3), (1, -2), (0, -1))
SHIFT = (1,)
FAR = len(SHIFT)
STEPS = 7
HOT_IN, HOT_SUM, HOT_OUT = 1, 3, 4


def kernel(
    sizes, ids_ref, hot_ref, grad_ref, cold_ref, hotg_ref,
    hc, mc, sb, rb, lt, lr, labs, dp, fw, bw, hs, hr, hp, hz, hq, hg, ho,
    ssem, rsem, lsend, lsem, zsend, fsem, bsem, hsem, sent, relay,
):
    ny, nzh, nx, nc, nzl = sizes
    np_, nz = ny * nx * nc, nzh * nzl
    tiles = ids_ref.shape[0]
    hot_rows = hs.shape[1]
    classes = hot_rows // 8
    group = np_ * 8
    y, zh, x, c, zl = (lax.axis_index(a) for a in AXES)
    me_p = (y * nx + x) * nc + c
    me_z = zh * nzl + zl
    sign = 1 - 2 * c

    def at(p, z):
        return (over(p, nx * nc), over(z, nzl), under(over(p, nc), nx), under(p, nc), under(z, nzl))

    def plane(p):
        return at(p, me_z)

    def column(z):
        return at(me_p, z)

    def mate(k):
        return under(me_p + k, np_)

    def above(k):
        return under(me_z + nz + k, nz)

    def remote(src, dst, send, recv, device):
        return pltpu.make_async_remote_copy(
            src_ref=src, dst_ref=dst, send_sem=send, recv_sem=recv,
            device_id=device, device_id_type=MESH,
        )

    def whole(ref, sem):
        pltpu.make_async_copy(ref, ref, sem).wait()

    barrier = pltpu.get_barrier_semaphore()

    def greet(sem, device):
        pl.semaphore_signal(sem, inc=1, device_id=device, device_id_type=MESH)

    greet(barrier, column(above(1)))
    greet(barrier, column(above(-1)))

    @pl.loop(1, np_)
    def _(k):
        greet(barrier, plane(mate(k)))

    def pass_on(r):
        greet(relay.at[r], column(above(2**r)))
        greet(relay.at[r], column(above(-(2**r))))

    idf = [ids_ref[k : k + 1, :].astype(F32) for k in range(tiles)]
    found = [jnp.zeros((8, 128), F32) for _ in range(tiles)]
    for i in range(hot_ref.shape[0]):
        row = hot_ref[i : i + 1, :].astype(F32)
        column_of = jnp.transpose(jnp.broadcast_to(row, (128, 128)))
        hc[i * 128 : (i + 1) * 128, :] = column_of
        for r in range(16):
            part = column_of[r * 8 : r * 8 + 8]
            found = [jnp.where(part == idf[k], 1.0, found[k]) for k in range(tiles)]

    cold = [
        jnp.where(jnp.max(found[k], axis=0, keepdims=True) > 0.0, -1.0, idf[k])
        for k in range(tiles)
    ]
    pair = lax.broadcasted_iota(I32, (np_ * 2, 128), 0)
    col = over(pair, 2)
    turn = 1 - 2 * under(col, nc)
    floors = []
    for near in NEAR:
        z = under(me_z + nz + turn * jnp.where(under(pair, 2) == 0, *near), nz)
        o = (over(col, nx * nc) * nzh + over(z, nzl)) * nx + under(over(col, nc), nx)
        o = (o * nc + under(col, nc)) * nzl + under(z, nzl)
        floors.append((o * ROWS).astype(F32))
    lows = [f - 1.0 for f in floors]
    for j in range(CAP):
        for s in range(len(NEAR)):
            low = jnp.where(cold[0] > lows[s], cold[0], BIG)
            for k in range(1, tiles):
                low = jnp.minimum(low, jnp.where(cold[k] > lows[s], cold[k], BIG))
            low = jnp.broadcast_to(jnp.min(low, axis=1, keepdims=True), pair.shape)
            lows[s] = jnp.where(low < floors[s] + float(ROWS), low, BIG)
            mc[pl.ds(s * group + j, np_ * 2, stride=CAP), :] = lows[s]

    lane = lax.broadcasted_iota(I32, (group, 128), 1)
    slot = under(lax.broadcasted_iota(I32, (group, 128), 0), 8)
    total = jnp.zeros((group, 128), F32)
    for s in range(len(NEAR)):
        low = mc[s * group : (s + 1) * group, :]
        value = jnp.where(low < BIG, under(low.astype(I32), ROWS).astype(F32) + 1.0, 0.0)
        total = jnp.where(lane == s * 8 + slot, value, total)
    lt[...] = jnp.sum(total.reshape(np_, 8, 128), axis=1, keepdims=True)

    grads = grad_ref[...]

    def slots(s):
        low = mc[pl.ds(pl.multiple_of(s * group, group), group), :]
        hits = [jnp.where(low == idf[k], 1.0, 0.0).astype(BF16) for k in range(tiles)]
        sums = jnp.dot(jnp.concatenate(hits, axis=1), grads, preferred_element_type=F32)
        sb[s] = sums.reshape(np_, 8, 128)

    for s in range(FAR + 1):
        slots(s)

    @pl.loop(0, hs.shape[0] * hot_rows // 128)
    def _(i):
        part = hc[pl.ds(pl.multiple_of(i * 128, 128), 128), :]
        hits = [jnp.where(part == idf[k], 1.0, 0.0).astype(BF16) for k in range(tiles)]
        sums = jnp.dot(jnp.concatenate(hits, axis=1), grads, preferred_element_type=F32)
        parts = 128 // hot_rows
        hs[pl.ds(i * parts, parts)] = sums.reshape(parts, hot_rows, 128)

    pl.semaphore_wait(barrier, 2 + np_ - 1)
    pass_on(0)

    def share(src, dst, send, recv):
        @pl.loop(1, np_)
        def _(k):
            p = mate(k)
            remote(src.at[p], dst.at[me_p], send, recv, plane(p)).start()

        pltpu.make_async_copy(src.at[me_p], dst.at[me_p], recv).start()

    def share_far(src, dst, send, recv, shift):
        @pl.loop(0, np_)
        def _(k):
            p = mate(k)
            z = above((1 - 2 * under(p, nc)) * shift)
            remote(src.at[p], dst.at[me_p], send, recv, at(p, z)).start()

    share(lt, lr.at[FAR], lsend.at[FAR], lsem.at[FAR])
    share(sb.at[FAR], rb.at[FAR], ssem.at[FAR], rsem.at[FAR])
    pl.semaphore_wait(relay.at[0], 2)
    pass_on(1)
    for s in range(FAR):
        share_far(lt, lr.at[s], lsend.at[s], lsem.at[s], SHIFT[s])
        share_far(sb.at[s], rb.at[s], ssem.at[s], rsem.at[s], SHIFT[s])

    def near(s):
        slots(s)
        share(sb.at[s], rb.at[s], ssem.at[s], rsem.at[s])

    near(FAR + 1)
    share(hs, hr, sent.at[1], hsem.at[0])
    pl.semaphore_wait(relay.at[1], 2)
    pass_on(2)

    @pl.loop(FAR + 2, len(NEAR))
    def _(s):
        near(s)

    for s in range(FAR + 1):
        whole(lr.at[s], lsem.at[s])
    lane = lax.broadcasted_iota(I32, (np_, 128), 1)
    known = lr[FAR].reshape(np_, 128)
    for s in range(FAR):
        known = jnp.where(over(lane, 8) == s, lr[s].reshape(np_, 128), known)
    spread = over(lax.broadcasted_iota(I32, (group, np_), 0), 8)
    spread = spread == lax.broadcasted_iota(I32, (group, np_), 1)
    wide = jnp.dot(
        jnp.where(spread, 1.0, 0.0).astype(BF16), known.astype(BF16), preferred_element_type=F32
    )
    lane = lax.broadcasted_iota(I32, (group, 128), 1)
    wide = jnp.where(under(lane, 8) == slot, wide, 0.0).astype(BF16)
    tile = over(lax.broadcasted_iota(I32, (8, 128), 1), 8)
    tile = tile == lax.broadcasted_iota(I32, (8, 128), 0)
    rows = lax.dot_general(
        jnp.where(tile, 1.0, 0.0).astype(BF16), wide, (((1,), (1,)), ((), ())),
        preferred_element_type=F32,
    )
    second = under(lax.broadcasted_iota(I32, (8, group), 1), 8) >= CAP
    labs[...] = jnp.where(rows > 0.0, rows - 1.0 + jnp.where(second, float(ROWS), 0.0), -1.0)

    def dense(s):
        whole(rb.at[s], rsem.at[s])
        values = rb[s].reshape(group, 128)
        high = values.astype(BF16)
        low = (values - high.astype(F32)).astype(BF16)
        where = lax.broadcasted_iota(I32, (2 * ROWS, group), 0).astype(F32)
        spread = jnp.where(labs[pl.ds(s, 1), :] == where, 1.0, 0.0).astype(BF16)
        both = jnp.dot(spread, jnp.concatenate([high, low], axis=1), preferred_element_type=F32)
        both = both[:, :128] + both[:, 128:]
        return both[:ROWS], both[ROWS:]

    piece = ROWS // SUB
    front, rear = column(above(sign)), column(above(-sign))
    main, side = pl.ds(0, ROWS), pl.ds(ROWS, ROWS)

    def send(i, j):
        part = pl.ds(j * piece, piece)
        other = pl.ds(ROWS + j * piece, piece)
        return (
            remote(dp.at[i, part], fw.at[i, part], zsend.at[0, i], fsem.at[i, j], front),
            remote(dp.at[i, other], bw.at[i, part], zsend.at[1, i], bsem.at[i, j], rear),
        )

    dp[0, main], dp[1, main] = dense(0)
    first, second = dense(1)
    dp[1, main] += first
    dp[0, side] = second
    for j in range(SUB):
        for copy in send(0, j):
            copy.start()
    dp[2, main], dp[1, side] = dense(2)

    family = me_z - under(me_z, classes)

    @pl.loop(1, STEPS)
    def _(i):
        for j in range(SUB):
            part = pl.ds(j * piece, piece)
            other = pl.ds(ROWS + j * piece, piece)
            ahead, behind = send(i, j)
            whole(fw.at[i - 1, part], fsem.at[i - 1, j])
            dp[i, part] += fw[i - 1, part]
            ahead.start()
            whole(bw.at[i - 1, part], bsem.at[i - 1, j])
            dp[i, other] += bw[i - 1, part]
            behind.start()

        @pl.when(i == HOT_IN)
        def _():
            whole(hr, hsem.at[0])

            def add_plane(k, total):
                return total + hr[k]

            total = lax.fori_loop(1, np_, add_plane, hr[0])
            hp[...] = total.reshape(classes, 8, 128)

            pl.semaphore_wait(relay.at[2], 2)

            @pl.loop(1, nz)
            def _(k):
                z = above(k)
                remote(hp.at[under(z, classes)], hz.at[me_z], sent.at[2], hsem.at[1], column(z)).start()

            pltpu.make_async_copy(hp.at[under(me_z, classes)], hz.at[me_z], hsem.at[1]).start()

        @pl.when(i == HOT_SUM)
        def _():
            whole(hz, hsem.at[1])
            total = hz[0]
            for k in range(1, nz):
                total += hz[k]
            hq[...] = total
            for k in range(1, classes):
                z = family + under(me_z + k, classes)
                here = hg.at[under(me_z, classes)]
                remote(hq, here, sent.at[3], hsem.at[2], column(z)).start()
            pltpu.make_async_copy(hq, hg.at[under(me_z, classes)], hsem.at[2]).start()

        @pl.when(i == HOT_OUT)
        def _():
            whole(hg, hsem.at[2])

            @pl.loop(1, np_)
            def _(k):
                remote(hg, ho.at[me_p], sent.at[4], hsem.at[3], plane(mate(k))).start()

            pltpu.make_async_copy(hg, ho.at[me_p], hsem.at[3]).start()

        @pl.when(i + 2 < len(NEAR))
        def _():
            dp[i + 2, main], dp[i + 1, side] = dense(i + 2)

    last = STEPS - 1
    for j in range(SUB):
        part = pl.ds(j * piece, piece)
        whole(fw.at[last, part], fsem.at[last, j])
        whole(bw.at[last, part], bsem.at[last, j])
        cold_ref[part, :] = dp[STEPS, part] + fw[last, part] + bw[last, part]
    whole(ho, hsem.at[3])
    hotg_ref[...] = ho[...].reshape(hotg_ref.shape)

    for s in range(FAR):
        whole(sb.at[s], ssem.at[s])
        whole(lt, lsend.at[s])
    whole(lt.at[pl.ds(0, np_ - 1)], lsend.at[FAR])

    @pl.loop(FAR, len(NEAR))
    def _(s):
        whole(sb.at[s, pl.ds(0, np_ - 1)], ssem.at[s])

    @pl.loop(0, STEPS)
    def _(i):
        whole(fw.at[i], zsend.at[0, i])
        whole(bw.at[i], zsend.at[1, i])

    whole(hs.at[pl.ds(0, np_ - 1)], sent.at[1])
    whole(hz.at[pl.ds(0, nz - 1)], sent.at[2])
    whole(hg.at[pl.ds(0, classes - 1)], sent.at[3])
    whole(ho.at[pl.ds(0, np_ - 1)], sent.at[4])


def adagrad(weights, moments, gradient):
    updated = moments + gradient * gradient
    return (weights - 0.5 * gradient / (jnp.sqrt(updated) + 1e-06), updated)


def body(sizes, gradients, row_ids, hot_ids, embedding, moments, hot_table, hot_moments):
    ny, nzh, nx, nc, nzl = sizes
    np_, nz = ny * nx * nc, nzh * nzl
    tiles = len(NEAR)
    hot_rows = hot_ids.shape[0] // np_
    classes = hot_rows // 8
    width = gradients.shape[1]
    vmem = pl.BlockSpec(memory_space=pltpu.VMEM)
    dma = pltpu.SemaphoreType.DMA
    cold_grad, hot_grad = pl.pallas_call(
        functools.partial(kernel, sizes),
        out_shape=(
            jax.ShapeDtypeStruct((ROWS, width), F32),
            jax.ShapeDtypeStruct((hot_ids.shape[0], width), F32),
        ),
        in_specs=[vmem] * 3,
        out_specs=(vmem, vmem),
        scratch_shapes=[
            pltpu.VMEM((hot_ids.shape[0], 128), F32),
            pltpu.VMEM((tiles * np_ * 8, 128), F32),
            pltpu.VMEM((tiles, np_, 8, 128), F32),
            pltpu.VMEM((tiles, np_, 8, 128), F32),
            pltpu.VMEM((np_, 1, 128), F32),
            pltpu.VMEM((FAR + 1, np_, 1, 128), F32),
            pltpu.VMEM((8, np_ * 8), F32),
            pltpu.VMEM((STEPS + 1, 2 * ROWS, 128), F32),
            pltpu.VMEM((STEPS, ROWS, 128), F32),
            pltpu.VMEM((STEPS, ROWS, 128), F32),
            pltpu.VMEM((np_, hot_rows, 128), F32),
            pltpu.VMEM((np_, hot_rows, 128), F32),
            pltpu.VMEM((classes, 8, 128), F32),
            pltpu.VMEM((nz, 8, 128), F32),
            pltpu.VMEM((8, 128), F32),
            pltpu.VMEM((classes, 8, 128), F32),
            pltpu.VMEM((np_, classes, 8, 128), F32),
            dma((tiles,)),
            dma((tiles,)),
            dma((FAR + 1,)),
            dma((FAR + 1,)),
            dma((2, STEPS)),
            dma((STEPS, SUB)),
            dma((STEPS, SUB)),
            dma((4,)),
            dma((5,)),
            pltpu.SemaphoreType.REGULAR((3,)),
        ],
        compiler_params=pltpu.CompilerParams(collective_id=0, has_side_effects=True),
    )(row_ids.reshape(-1, 128), hot_ids.reshape(-1, 128), gradients)
    new_table, new_moments = adagrad(embedding, moments, cold_grad)
    new_hot_table, new_hot_moments = adagrad(hot_table, hot_moments, hot_grad)
    return (new_table, new_moments, new_hot_table, new_hot_moments)


def program(torus):
    sizes = tuple(torus.shape[a] for a in AXES)
    rows = P(AXES, None)
    return jax.shard_map(
        functools.partial(body, sizes),
        mesh=torus,
        in_specs=(rows, P(AXES), P(), rows, rows, P(), P()),
        out_specs=(rows, rows, P(), P()),
        check_vma=False,
    )


def solution(mesh):
    shape = (mesh.shape["gx"] // 2, 2, mesh.shape["gy"] // 2, 2, mesh.shape["gz"])
    return program(Mesh(mesh.devices.reshape(shape), AXES))
```

```python
import functools

import jax
import jax.numpy as jnp
from jax import lax
from jax.experimental import pallas as pl
from jax.experimental.pallas import tpu as pltpu
from jax.sharding import Mesh
from jax.sharding import PartitionSpec as P

AXES = ("gx_0", "gx_1", "gy_0", "gy_1", "gz")
CAP = 4
ROWS = 256
BIG = 1.0e9
SUB = 4
MESH = pl.DeviceIdType.MESH
F32, BF16, I32 = jnp.float32, jnp.bfloat16, jnp.int32


def half_of(n):
    return n.bit_length() - 1


def over(v, n):
    return v >> half_of(n)


def under(v, n):
    return v & (n - 1)


NEAR = ((8, 7), (6, -7), (5, -6), (4, -5), (3, -4), (2, -3), (1, -2), (0, -1))
SHIFT = (1,)
FAR = len(SHIFT)
STEPS = 7
HOT_IN, HOT_SUM, HOT_OUT = 1, 3, 4


def kernel(
    sizes, ids_ref, hot_ref, grad_ref, cold_ref, hotg_ref,
    hc, mc, sb, rb, lt, lr, labs, dp, fw, bw, hs, hr, hp, hz, hq, hg, ho,
    ssem, rsem, lsend, lsem, zsend, fsem, bsem, hsem, sent, relay,
):
    ny, nzh, nx, nc, nzl = sizes
    np_, nz = ny * nx * nc, nzh * nzl
    tiles = ids_ref.shape[0]
    hot_rows = hs.shape[1]
    classes = hot_rows // 8
    group = np_ * 8
    y, zh, x, c, zl = (lax.axis_index(a) for a in AXES)
    me_p = (y * nx + x) * nc + c
    me_z = zh * nzl + zl
    sign = 1 - 2 * c

    def at(p, z):
        return (over(p, nx * nc), over(z, nzl), under(over(p, nc), nx), under(p, nc), under(z, nzl))

    def plane(p):
        return at(p, me_z)

    def column(z):
        return at(me_p, z)

    def mate(k):
        return under(me_p + k, np_)

    def above(k):
        return under(me_z + nz + k, nz)

    def remote(src, dst, send, recv, device):
        return pltpu.make_async_remote_copy(
            src_ref=src, dst_ref=dst, send_sem=send, recv_sem=recv,
            device_id=device, device_id_type=MESH,
        )

    def whole(ref, sem):
        pltpu.make_async_copy(ref, ref, sem).wait()

    barrier = pltpu.get_barrier_semaphore()

    def greet(sem, device):
        pl.semaphore_signal(sem, inc=1, device_id=device, device_id_type=MESH)

    greet(barrier, column(above(1)))
    greet(barrier, column(above(-1)))

    @pl.loop(1, np_)
    def _(k):
        greet(barrier, plane(mate(k)))

    def pass_on(r):
        greet(relay.at[r], column(above(2**r)))
        greet(relay.at[r], column(above(-(2**r))))

    idf = [ids_ref[k : k + 1, :].astype(F32) for k in range(tiles)]
    found = [jnp.zeros((8, 128), F32) for _ in range(tiles)]
    for i in range(hot_ref.shape[0]):
        row = hot_ref[i : i + 1, :].astype(F32)
        column_of = jnp.transpose(jnp.broadcast_to(row, (128, 128)))
        hc[i * 128 : (i + 1) * 128, :] = column_of
        for r in range(16):
            part = column_of[r * 8 : r * 8 + 8]
            found = [jnp.where(part == idf[k], 1.0, found[k]) for k in range(tiles)]

    cold = [
        jnp.where(jnp.max(found[k], axis=0, keepdims=True) > 0.0, -1.0, idf[k])
        for k in range(tiles)
    ]
    pair = lax.broadcasted_iota(I32, (np_ * 2, 128), 0)
    col = over(pair, 2)
    turn = 1 - 2 * under(col, nc)
    floors = []
    for near in NEAR:
        z = under(me_z + nz + turn * jnp.where(under(pair, 2) == 0, *near), nz)
        o = (over(col, nx * nc) * nzh + over(z, nzl)) * nx + under(over(col, nc), nx)
        o = (o * nc + under(col, nc)) * nzl + under(z, nzl)
        floors.append((o * ROWS).astype(F32))
    lows = [f - 1.0 for f in floors]
    for j in range(CAP):
        for s in range(len(NEAR)):
            low = jnp.where(cold[0] > lows[s], cold[0], BIG)
            for k in range(1, tiles):
                low = jnp.minimum(low, jnp.where(cold[k] > lows[s], cold[k], BIG))
            low = jnp.broadcast_to(jnp.min(low, axis=1, keepdims=True), pair.shape)
            lows[s] = jnp.where(low < floors[s] + float(ROWS), low, BIG)
            mc[pl.ds(s * group + j, np_ * 2, stride=CAP), :] = lows[s]

    lane = lax.broadcasted_iota(I32, (group, 128), 1)
    slot = under(lax.broadcasted_iota(I32, (group, 128), 0), 8)
    total = jnp.zeros((group, 128), F32)
    for s in range(len(NEAR)):
        low = mc[s * group : (s + 1) * group, :]
        value = jnp.where(low < BIG, under(low.astype(I32), ROWS).astype(F32) + 1.0, 0.0)
        total = jnp.where(lane == s * 8 + slot, value, total)
    lt[...] = jnp.sum(total.reshape(np_, 8, 128), axis=1, keepdims=True)

    grads = grad_ref[...]

    def slots(s):
        low = mc[pl.ds(pl.multiple_of(s * group, group), group), :]
        hits = [jnp.where(low == idf[k], 1.0, 0.0).astype(BF16) for k in range(tiles)]
        sums = jnp.dot(jnp.concatenate(hits, axis=1), grads, preferred_element_type=F32)
        sb[s] = sums.reshape(np_, 8, 128)

    for s in range(FAR + 1):
        slots(s)

    @pl.loop(0, hs.shape[0] * hot_rows // 128)
    def _(i):
        part = hc[pl.ds(pl.multiple_of(i * 128, 128), 128), :]
        hits = [jnp.where(part == idf[k], 1.0, 0.0).astype(BF16) for k in range(tiles)]
        sums = jnp.dot(jnp.concatenate(hits, axis=1), grads, preferred_element_type=F32)
        parts = 128 // hot_rows
        hs[pl.ds(i * parts, parts)] = sums.reshape(parts, hot_rows, 128)

    pl.semaphore_wait(barrier, 2 + np_ - 1)
    pass_on(0)

    def share(src, dst, send, recv):
        @pl.loop(1, np_)
        def _(k):
            p = mate(k)
            remote(src.at[p], dst.at[me_p], send, recv, plane(p)).start()

        pltpu.make_async_copy(src.at[me_p], dst.at[me_p], recv).start()

    def share_far(src, dst, send, recv, shift):
        @pl.loop(0, np_)
        def _(k):
            p = mate(k)
            z = above((1 - 2 * under(p, nc)) * shift)
            remote(src.at[p], dst.at[me_p], send, recv, at(p, z)).start()

    share(lt, lr.at[FAR], lsend.at[FAR], lsem.at[FAR])
    share(sb.at[FAR], rb.at[FAR], ssem.at[FAR], rsem.at[FAR])
    pl.semaphore_wait(relay.at[0], 2)
    pass_on(1)
    for s in range(FAR):
        share_far(lt, lr.at[s], lsend.at[s], lsem.at[s], SHIFT[s])
        share_far(sb.at[s], rb.at[s], ssem.at[s], rsem.at[s], SHIFT[s])

    def near(s):
        slots(s)
        share(sb.at[s], rb.at[s], ssem.at[s], rsem.at[s])

    near(FAR + 1)
    share(hs, hr, sent.at[1], hsem.at[0])
    pl.semaphore_wait(relay.at[1], 2)
    pass_on(2)

    near(FAR + 2)

    for s in range(FAR + 1):
        whole(lr.at[s], lsem.at[s])
    lane = lax.broadcasted_iota(I32, (np_, 128), 1)
    known = lr[FAR].reshape(np_, 128)
    for s in range(FAR):
        known = jnp.where(over(lane, 8) == s, lr[s].reshape(np_, 128), known)
    spread = over(lax.broadcasted_iota(I32, (group, np_), 0), 8)
    spread = spread == lax.broadcasted_iota(I32, (group, np_), 1)
    wide = jnp.dot(
        jnp.where(spread, 1.0, 0.0).astype(BF16), known.astype(BF16), preferred_element_type=F32
    )
    lane = lax.broadcasted_iota(I32, (group, 128), 1)
    wide = jnp.where(under(lane, 8) == slot, wide, 0.0).astype(BF16)
    tile = over(lax.broadcasted_iota(I32, (8, 128), 1), 8)
    tile = tile == lax.broadcasted_iota(I32, (8, 128), 0)
    rows = lax.dot_general(
        jnp.where(tile, 1.0, 0.0).astype(BF16), wide, (((1,), (1,)), ((), ())),
        preferred_element_type=F32,
    )
    second = under(lax.broadcasted_iota(I32, (8, group), 1), 8) >= CAP
    labs[...] = jnp.where(rows > 0.0, rows - 1.0 + jnp.where(second, float(ROWS), 0.0), -1.0)

    def dense(s):
        whole(rb.at[s], rsem.at[s])
        values = rb[s].reshape(group, 128)
        high = values.astype(BF16)
        low = (values - high.astype(F32)).astype(BF16)
        where = lax.broadcasted_iota(I32, (2 * ROWS, group), 0).astype(F32)
        spread = jnp.where(labs[pl.ds(s, 1), :] == where, 1.0, 0.0).astype(BF16)
        both = jnp.dot(spread, jnp.concatenate([high, low], axis=1), preferred_element_type=F32)
        both = both[:, :128] + both[:, 128:]
        return both[:ROWS], both[ROWS:]

    piece = ROWS // SUB
    front, rear = column(above(sign)), column(above(-sign))
    main, side = pl.ds(0, ROWS), pl.ds(ROWS, ROWS)

    def send(i, j):
        part = pl.ds(j * piece, piece)
        other = pl.ds(ROWS + j * piece, piece)
        return (
            remote(dp.at[i, part], fw.at[i, part], zsend.at[0, i], fsem.at[i, j], front),
            remote(dp.at[i, other], bw.at[i, part], zsend.at[1, i], bsem.at[i, j], rear),
        )

    dp[0, main], dp[1, main] = dense(0)
    first, second = dense(1)
    dp[1, main] += first
    dp[0, side] = second
    for j in range(SUB):
        for copy in send(0, j):
            copy.start()
    near(FAR + 3)
    dp[2, main], dp[1, side] = dense(2)

    family = me_z - under(me_z, classes)

    @pl.loop(1, STEPS)
    def _(i):
        for j in range(SUB):
            part = pl.ds(j * piece, piece)
            other = pl.ds(ROWS + j * piece, piece)
            ahead, behind = send(i, j)
            whole(fw.at[i - 1, part], fsem.at[i - 1, j])
            dp[i, part] += fw[i - 1, part]
            ahead.start()
            whole(bw.at[i - 1, part], bsem.at[i - 1, j])
            dp[i, other] += bw[i - 1, part]
            behind.start()

        @pl.when(i + FAR + 3 < len(NEAR))
        def _():
            near(i + FAR + 3)

        @pl.when(i + 2 < len(NEAR))
        def _():
            dp[i + 2, main], dp[i + 1, side] = dense(i + 2)

        @pl.when(i == HOT_IN)
        def _():
            whole(hr, hsem.at[0])

            def add_plane(k, total):
                return total + hr[k]

            total = lax.fori_loop(1, np_, add_plane, hr[0])
            hp[...] = total.reshape(classes, 8, 128)

            pl.semaphore_wait(relay.at[2], 2)

            @pl.loop(1, nz)
            def _(k):
                z = above(k)
                remote(hp.at[under(z, classes)], hz.at[me_z], sent.at[2], hsem.at[1], column(z)).start()

            pltpu.make_async_copy(hp.at[under(me_z, classes)], hz.at[me_z], hsem.at[1]).start()

        @pl.when(i == HOT_SUM)
        def _():
            whole(hz, hsem.at[1])
            total = hz[0]
            for k in range(1, nz):
                total += hz[k]
            hq[...] = total
            for k in range(1, classes):
                z = family + under(me_z + k, classes)
                here = hg.at[under(me_z, classes)]
                remote(hq, here, sent.at[3], hsem.at[2], column(z)).start()
            pltpu.make_async_copy(hq, hg.at[under(me_z, classes)], hsem.at[2]).start()

        @pl.when(i == HOT_OUT)
        def _():
            whole(hg, hsem.at[2])

            @pl.loop(1, np_)
            def _(k):
                remote(hg, ho.at[me_p], sent.at[4], hsem.at[3], plane(mate(k))).start()

            pltpu.make_async_copy(hg, ho.at[me_p], hsem.at[3]).start()

    last = STEPS - 1
    for j in range(SUB):
        part = pl.ds(j * piece, piece)
        whole(fw.at[last, part], fsem.at[last, j])
        whole(bw.at[last, part], bsem.at[last, j])
        cold_ref[part, :] = dp[STEPS, part] + fw[last, part] + bw[last, part]
    whole(ho, hsem.at[3])
    hotg_ref[...] = ho[...].reshape(hotg_ref.shape)

    for s in range(FAR):
        whole(sb.at[s], ssem.at[s])
        whole(lt, lsend.at[s])
    whole(lt.at[pl.ds(0, np_ - 1)], lsend.at[FAR])

    @pl.loop(FAR, len(NEAR))
    def _(s):
        whole(sb.at[s, pl.ds(0, np_ - 1)], ssem.at[s])

    @pl.loop(0, STEPS)
    def _(i):
        whole(fw.at[i], zsend.at[0, i])
        whole(bw.at[i], zsend.at[1, i])

    whole(hs.at[pl.ds(0, np_ - 1)], sent.at[1])
    whole(hz.at[pl.ds(0, nz - 1)], sent.at[2])
    whole(hg.at[pl.ds(0, classes - 1)], sent.at[3])
    whole(ho.at[pl.ds(0, np_ - 1)], sent.at[4])


def adagrad(weights, moments, gradient):
    updated = moments + gradient * gradient
    return (weights - 0.5 * gradient / (jnp.sqrt(updated) + 1e-06), updated)


def body(sizes, gradients, row_ids, hot_ids, embedding, moments, hot_table, hot_moments):
    ny, nzh, nx, nc, nzl = sizes
    np_, nz = ny * nx * nc, nzh * nzl
    tiles = len(NEAR)
    hot_rows = hot_ids.shape[0] // np_
    classes = hot_rows // 8
    width = gradients.shape[1]
    vmem = pl.BlockSpec(memory_space=pltpu.VMEM)
    dma = pltpu.SemaphoreType.DMA
    cold_grad, hot_grad = pl.pallas_call(
        functools.partial(kernel, sizes),
        out_shape=(
            jax.ShapeDtypeStruct((ROWS, width), F32),
            jax.ShapeDtypeStruct((hot_ids.shape[0], width), F32),
        ),
        in_specs=[vmem] * 3,
        out_specs=(vmem, vmem),
        scratch_shapes=[
            pltpu.VMEM((hot_ids.shape[0], 128), F32),
            pltpu.VMEM((tiles * np_ * 8, 128), F32),
            pltpu.VMEM((tiles, np_, 8, 128), F32),
            pltpu.VMEM((tiles, np_, 8, 128), F32),
            pltpu.VMEM((np_, 1, 128), F32),
            pltpu.VMEM((FAR + 1, np_, 1, 128), F32),
            pltpu.VMEM((8, np_ * 8), F32),
            pltpu.VMEM((STEPS + 1, 2 * ROWS, 128), F32),
            pltpu.VMEM((STEPS, ROWS, 128), F32),
            pltpu.VMEM((STEPS, ROWS, 128), F32),
            pltpu.VMEM((np_, hot_rows, 128), F32),
            pltpu.VMEM((np_, hot_rows, 128), F32),
            pltpu.VMEM((classes, 8, 128), F32),
            pltpu.VMEM((nz, 8, 128), F32),
            pltpu.VMEM((8, 128), F32),
            pltpu.VMEM((classes, 8, 128), F32),
            pltpu.VMEM((np_, classes, 8, 128), F32),
            dma((tiles,)),
            dma((tiles,)),
            dma((FAR + 1,)),
            dma((FAR + 1,)),
            dma((2, STEPS)),
            dma((STEPS, SUB)),
            dma((STEPS, SUB)),
            dma((4,)),
            dma((5,)),
            pltpu.SemaphoreType.REGULAR((3,)),
        ],
        compiler_params=pltpu.CompilerParams(collective_id=0, has_side_effects=True),
    )(row_ids.reshape(-1, 128), hot_ids.reshape(-1, 128), gradients)
    new_table, new_moments = adagrad(embedding, moments, cold_grad)
    new_hot_table, new_hot_moments = adagrad(hot_table, hot_moments, hot_grad)
    return (new_table, new_moments, new_hot_table, new_hot_moments)


def program(torus):
    sizes = tuple(torus.shape[a] for a in AXES)
    rows = P(AXES, None)
    return jax.shard_map(
        functools.partial(body, sizes),
        mesh=torus,
        in_specs=(rows, P(AXES), P(), rows, rows, P(), P()),
        out_specs=(rows, rows, P(), P()),
        check_vma=False,
    )


def solution(mesh):
    shape = (mesh.shape["gx"] // 2, 2, mesh.shape["gy"] // 2, 2, mesh.shape["gz"])
    return program(Mesh(mesh.devices.reshape(shape), AXES))
```
